32 devices in a mesh: kpool: 8 (over y, x, core), band: 4 (over z).
Axes of the slice: x: 2, y: 2, z: 4, core: 2. Of those that a mesh axis runs over, the one named last changes fastest.
Arguments:
- psi: bfloat16 [8, 2, 4, 48, 2304], P('kpool', None, 'band'), may hold values from -6 to 6
- kpoint_of_pool: int32 [8], replicated, may hold values from 0 to 7, each once
Outputs:
- exchange: float32 [8, 2, 4, 48, 2304], P('kpool', None, 'band')
The draws below stay inside these ranges and needn't reach their ends.
Inputs may be any that keep to these rules, and one draw needn't show every extreme that they name: `kpoint_of_pool`: each value appears once.
All inputs are finite; a program needn't handle non-finite values.
Results may differ from the reference program's by a relative error of at most 0.0003.
Values may be sent and summed in bfloat16 or wider, within the bound.
A program may use at most 64 MiB of HBM per device.

```python
import jax
import jax.numpy as jnp
from jax import lax

GRID = 48
KMESH = 4
ROUNDS = 1
NK = 8
BLOCK = 4


def levels(stream_key, shape, split, smallest, top_value):
    def one(axis_at, parts):
        draws = jax.random.uniform(jax.random.fold_in(jax.random.fold_in(stream_key, 6), axis_at), (parts,), jnp.float32, smallest / len(split), top_value / len(split))
        return jnp.repeat(jnp.exp(draws), shape[axis_at] // parts).reshape((-1,) + (1,) * (len(shape) - axis_at - 1))

    loudness = one(*split[0])
    for cut in split[1:]:
        loudness = loudness * one(*cut)
    return loudness


def normal_values(stream_key, extent, deviation, limit, shards=(), kind=jnp.bfloat16):
    values = jax.random.normal(stream_key, extent, jnp.float32) * deviation
    if len(shards) > 0:
        values = levels(stream_key, extent, shards, -0.22, 0.18) * values
    return jnp.clip(values, min=-limit, max=limit).astype(kind)


def setup_inputs(seed: int = 0) -> dict:
    splits = jax.random.split(jax.random.key(seed), 3)
    psi = normal_values(splits[0], (NK, 2, BLOCK, GRID, GRID * GRID), 1.0, 6.0, ((0, 8), (2, 4)))
    kpoint_of_pool = jax.random.permutation(splits[1], NK).astype(jnp.int32)
    return {"psi": psi, "kpoint_of_pool": kpoint_of_pool}


def kpoint_coords(labels):
    first = labels % KMESH
    second = (labels // KMESH) % KMESH
    third = labels // (KMESH * KMESH)
    return jnp.stack([first, second, third], axis=1).astype(jnp.float32) / KMESH


def coulomb(offset):
    index = jnp.arange(GRID, dtype=jnp.int32)
    freq = jnp.where(index < GRID // 2, index, index - GRID).astype(jnp.float32)
    edge = index == GRID // 2
    along_x = (offset[0] + freq) ** 2
    along_y = (offset[1] + freq) ** 2
    along_z = (offset[2] + freq) ** 2
    squared = along_x[:, None, None] + along_y[None, :, None] + along_z[None, None, :]
    cutoff = edge[:, None, None] | edge[None, :, None] | edge[None, None, :]
    safe = jnp.where(cutoff, 1.0, squared)
    amplitude = GRID ** 1.5 / 16.0
    return jnp.where(cutoff, 0.0, amplitude / safe)


def reference(psi, kpoint_of_pool):
    orbitals = lax.complex(psi[:, 0].astype(jnp.float32), psi[:, 1].astype(jnp.float32))
    orbitals = orbitals.reshape(NK, BLOCK, GRID, GRID, GRID)
    coords = kpoint_coords(kpoint_of_pool)
    weight = -(2.0 * ROUNDS * BLOCK) ** -0.5
    npoints = GRID * GRID * GRID

    def one_pool(pool):
        own = orbitals[pool]
        total = jnp.zeros_like(own)
        for turn in range(1, ROUNDS + 1):
            for direction in (1, -1):
                partner = (pool - direction * turn) % NK
                other = orbitals[partner]
                kernel = coulomb(coords[pool] - coords[partner])
                density = jnp.conj(other)[None] * own[:, None]
                spectrum = jnp.fft.fftn(density, axes=(2, 3, 4)) / npoints
                potential = jnp.fft.ifftn(spectrum * kernel, axes=(2, 3, 4)) * npoints
                total = total + jnp.sum(other[None] * potential, axis=1)
        total = total * weight
        return jnp.stack([jnp.real(total), jnp.imag(total)]).reshape(2, BLOCK, GRID, GRID * GRID)

    return lax.map(one_pool, jnp.arange(NK, dtype=jnp.int32))
```

```python
import functools
import math

import jax
import jax.numpy as jnp
import numpy as np
from jax import lax
from jax.experimental import pallas as pl
from jax.experimental.pallas import tpu as pltpu
from jax.sharding import PartitionSpec as P

KMESH = 4
ROUNDS = 1
LANES = 128
HALF = 64
PITCH = 8
MESH = pl.DeviceIdType.MESH


def kpoint_coords(labels):
    first = labels % KMESH
    second = labels // KMESH % KMESH
    third = labels // (KMESH * KMESH)
    return jnp.stack([first, second, third], axis=1).astype(jnp.float32) / KMESH


def two_parts(table):
    high = table.astype(jnp.bfloat16)
    low = (table - high.astype(np.float32)).astype(jnp.bfloat16)
    return high, low


def dft_tables(grid):
    index = np.arange(grid)
    angles = (index[:, None] * index[None, :] % grid) * (2.0 * math.pi / grid)
    cosine = np.cos(angles).astype(np.float32)
    sine = np.sin(angles).astype(np.float32)
    lanes = []
    for sign in (1.0, -1.0):
        full = np.zeros((LANES, LANES), np.float32)
        full[:grid, :grid] = cosine
        full[HALF : HALF + grid, HALF : HALF + grid] = cosine
        full[:grid, HALF : HALF + grid] = -sign * sine
        full[HALF : HALF + grid, :grid] = sign * sine
        high, low = two_parts(full)
        lanes.append(np.block([[high, low], [high, np.zeros_like(low)]]))
    high, low = two_parts(np.concatenate([cosine, sine], axis=0))
    rows = np.concatenate([high, high, low], axis=1)
    return np.stack(lanes), rows


def split(x):
    high = x.astype(jnp.bfloat16)
    low = (x - high.astype(jnp.float32)).astype(jnp.bfloat16)
    return high, low


def visits(ring, n):
    return [n] + sorted((m for m in range(ring) if m != n), key=lambda m: (abs(m - n), (m - n) % 2 * 0 + (m ^ 1 != n)))


def squares(offset, grid, axis_len):
    index = jnp.arange(axis_len, dtype=jnp.int32) % (HALF if axis_len > grid else grid)
    freq = jnp.where(index < grid // 2, index, index - grid).astype(jnp.float32)
    cut = (index == grid // 2) | (index >= grid)
    return jnp.where(cut, 1e30, (offset + freq) ** 2)


def kernel(grid, ring, pools, pitch, sent_ref, a1_ref, a2_ref, ax_ref, ay_ref, az_ref, lanes_ref, rows_ref, out_ref,
           bufs, field, acc1, acc2, v_ref, recv_sem, send_sem):
    points = grid * grid
    packed = sent_ref.shape[0]
    quarter = points - packed
    me, n = lax.axis_index("kpool"), lax.axis_index("band")
    odd = me % 2
    turn = 1 - 2 * odd
    near = (me + turn + pools) % pools
    far = (me - turn + pools) % pools
    beyond = (me + 2 * turn + pools) % pools
    before = (me - 2 * turn + pools) % pools

    barrier = pltpu.get_barrier_semaphore()

    def hail(pool, band):
        pl.semaphore_signal(barrier, inc=1, device_id=(pool, band), device_id_type=MESH)

    for pool in (near, far, beyond, before):
        hail(pool, n)
    for plane in range(ring):
        @pl.when(n == plane)
        def _():
            count = 4
            for other in (plane - 1, plane + 1):
                if 0 <= other < ring:
                    hail(near, other)
                    hail(me, other)
                    count += 2
            pl.semaphore_wait(barrier, count)

    def place(plane, band, outer):
        return 2 * visits(ring, plane).index(band) + outer

    def copy(source, step, pool, band, slot):
        return pltpu.make_async_remote_copy(
            src_ref=source,
            dst_ref=bufs.at[step, pl.ds(0, packed)],
            send_sem=send_sem.at[slot],
            recv_sem=recv_sem.at[step],
            device_id=(pool, band),
            device_id_type=MESH,
        )

    def sends(plane):
        first = [(sent_ref, place(plane, plane, 0), near, plane, 0)]
        first.append((sent_ref, place(plane, plane, 1), far, plane, 1))
        slot = 2
        for other in (plane - 1, plane + 1):
            if 0 <= other < ring:
                first.append((sent_ref, place(other, plane, 0), near, other, slot))
                slot += 1
        later = {}
        for band in visits(ring, plane)[1:]:
            step = place(plane, band, 0)
            source = bufs.at[step, pl.ds(0, packed)]
            onward = plane + 1 if band < plane else plane - 1
            copies = []
            if 0 <= onward < ring:
                copies.append((source, place(onward, band, 0), me, onward, slot))
                slot += 1
            copies.append((source, place(plane, band, 1), beyond, plane, slot))
            slot += 1
            later[step] = copies
        return first, later

    def arrival(step):
        spot = bufs.at[step, pl.ds(0, packed)]
        pltpu.make_async_copy(spot, spot, recv_sem.at[step]).wait()

    def service(step, moment):
        for plane in range(ring):
            order = visits(ring, plane)
            due = []
            for at, band in enumerate(order):
                if at == 0:
                    continue
                when = 1 if abs(band - plane) == 1 else 2 * at - 1
                due.append((when, 2 * at))

            @pl.when(n == plane)
            def _():
                for when, number in due:
                    @pl.when(moment == when)
                    def _():
                        arrival(number)
                        for c in sends(plane)[1][number]:
                            copy(*c).start()

    for plane in range(ring):
        @pl.when(n == plane)
        def _():
            for c in sends(plane)[0]:
                copy(*c).start()

    lane = lax.broadcasted_iota(jnp.int32, (1, LANES), 1)
    sign = jnp.where(lane < HALF, 1.0, -1.0).astype(jnp.float32)
    scale = grid**1.5 / 16.0 / (grid * grid * grid)

    def make_v(y, carry):
        for which in range(2):
            total = ax_ref[which] + ay_ref[which, pl.ds(y, 1), :] + az_ref[which, 0:1, :]
            v_ref[which, y] = jnp.where(total > 1e29, 0.0, scale / total)
        return carry

    lax.fori_loop(0, grid, make_v, 0)

    def swap(x):
        return pltpu.roll(x, HALF, 1)

    def turned(x):
        return swap(x) * sign

    def along_lanes(x, which):
        high, low = split(x)
        out = jnp.dot(
            jnp.concatenate([high, low], axis=1), lanes_ref[which], preferred_element_type=jnp.float32
        )
        return out[:, :LANES] + out[:, LANES:]

    def along_rows(xs, sense):
        parts = []
        for x in xs:
            high, low = split(x)
            parts.append(jnp.concatenate([high, low, high], axis=0))
        outs = []
        for at in range(0, len(parts), 2):
            pair = jnp.concatenate(parts[at : at + 2], axis=1)
            out = jnp.dot(rows_ref[...], pair, preferred_element_type=jnp.float32)
            for j in range(len(parts[at : at + 2])):
                piece = out[:, j * LANES : (j + 1) * LANES]
                q = turned(piece[grid:])
                outs.append(piece[:grid] + q if sense > 0 else piece[:grid] - q)
        return outs

    def one_field(step, carry):
        @pl.when(step % 2 == 1)
        def _():
            service(step, step)

        @pl.when(jnp.logical_or(step == 0, step % 2 == 1))
        def _():
            arrival(step)

        which = step % 2
        spread = lane % HALF // 16

        def unstuff(at, carry):
            rows = 48
            total = jnp.zeros((rows, LANES), jnp.float32)
            for c in range(3):
                x = bufs[step, pl.ds(pl.multiple_of(c * quarter + at * rows, 16), rows), :].astype(jnp.float32)
                total = jnp.where(spread == c, pltpu.roll(x, (c * 16 - 48) % LANES, 1), total)
            bufs[step, pl.ds(pl.multiple_of(packed + at * rows, 16), rows), :] = total.astype(jnp.bfloat16)
            return carry

        lax.fori_loop(0, quarter // 48, unstuff, 0)

        def band_rows(x):
            return bufs[step, x * grid : (x + 1) * grid, :].astype(jnp.float32)

        for base in range(0, grid, 4):
            dens = []
            for x in range(base, base + 4):
                b = band_rows(x)
                span = slice(x * grid, (x + 1) * grid)
                dens.append(b * a1_ref[span, :] + swap(b) * a2_ref[span, :])
            spec = along_lanes(jnp.concatenate(dens, axis=0), 0)
            outs = along_rows([spec[j * grid : (j + 1) * grid] for j in range(4)], 1)
            for j in range(4):
                field[(base + j) * pitch : (base + j) * pitch + grid, :] = outs[j]

        for base in range(0, grid, 4):
            xs = [field[pl.ds(base + j, grid, stride=pitch), :] for j in range(4)]
            spec = along_rows(xs, 1)
            spec = [spec[j] * v_ref[which, base + j] for j in range(4)]
            outs = along_rows(spec, -1)
            for j in range(4):
                field[pl.ds(base + j, grid, stride=pitch), :] = outs[j]

        for base in range(0, grid, 4):
            mids = [field[(base + j) * pitch : (base + j) * pitch + grid, :] for j in range(4)]
            outs = along_rows(mids, -1)
            pot = along_lanes(jnp.concatenate(outs, axis=0), 1)
            for j in range(4):
                x = base + j
                b = band_rows(x)
                span = slice(x * grid, (x + 1) * grid)
                piece = pot[j * grid : (j + 1) * grid]
                acc1[span, :] = acc1[span, :] + b * piece
                acc2[span, :] = acc2[span, :] + b * swap(piece)
        return carry

    acc1[...] = jnp.zeros_like(acc1)
    acc2[...] = jnp.zeros_like(acc2)
    lax.fori_loop(0, 2 * ring, one_field, 0)

    weight = -((2.0 * ROUNDS * ring) ** (-0.5))
    first = lane < HALF

    def finish(x, carry):
        rows = pl.ds(pl.multiple_of(x * grid, 16), grid)
        one = acc1[rows, :]
        two = acc2[rows, :]
        real = one - swap(one)
        imag = two + swap(two)
        out_ref[rows, :] = jnp.where(first, real, imag) * weight
        return carry

    lax.fori_loop(0, grid, finish, 0)

    for plane in range(ring):
        @pl.when(n == plane)
        def _():
            begun, later = sends(plane)
            for c in begun:
                copy(*c).wait_send()
            for copies in later.values():
                for c in copies:
                    copy(*c).wait_send()


def per_device(psi, kpoint_of_pool):
    own = psi[0, :, 0]
    grid = own.shape[1]
    ring = lax.axis_size("band")
    pools = lax.axis_size("kpool")
    me = lax.axis_index("kpool")
    coords = kpoint_coords(kpoint_of_pool)
    turn = 1 - 2 * (me % 2)
    here = lax.dynamic_index_in_dim(coords, me, 0, keepdims=False)
    offsets = jnp.stack(
        [
            here - lax.dynamic_index_in_dim(coords, (me + turn + pools) % pools, 0, keepdims=False),
            here - lax.dynamic_index_in_dim(coords, (me - turn + pools) % pools, 0, keepdims=False),
        ]
    )
    along = jax.vmap(lambda o: squares(o, grid, grid))
    ax = jnp.broadcast_to(along(offsets[:, 0])[:, :, None], (2, grid, LANES))
    ay = jnp.broadcast_to(along(offsets[:, 1])[:, :, None], (2, grid, LANES))
    az = jax.vmap(lambda o: squares(o, grid, LANES))(offsets[:, 2])
    az = jnp.broadcast_to(az[:, None, :], (2, 8, LANES))
    points = grid * grid
    kept = grid * 3 // 4
    parts = own.reshape(2, grid, grid, grid)
    extra = parts[:, kept:].reshape(2, grid - kept, grid, 3, 16)
    extra = jnp.moveaxis(extra, 3, 1).reshape(2, kept, grid, 16)
    stuffed = jnp.concatenate([parts[:, :kept], extra], axis=-1)
    stuffed = jnp.concatenate([stuffed[0], stuffed[1]], axis=-1).reshape(kept * grid, LANES)
    wide = jnp.pad(parts.reshape(2, points, grid), ((0, 0), (0, 0), (0, HALF - grid))).astype(jnp.float32)
    a1 = jnp.concatenate([wide[0], -wide[0]], axis=-1)
    a2 = jnp.concatenate([wide[1], wide[1]], axis=-1)
    lanes, rows = dft_tables(grid)
    whole = pl.BlockSpec(memory_space=pltpu.VMEM)
    args = [stuffed, a1, a2, ax, ay, az, jnp.asarray(lanes), jnp.asarray(rows)]
    pitch = grid + PITCH
    total = pl.pallas_call(
        functools.partial(kernel, grid, ring, pools, pitch),
        in_specs=[whole] * len(args),
        out_specs=whole,
        out_shape=jax.ShapeDtypeStruct((points, LANES), jnp.float32),
        scratch_shapes=[
            pltpu.VMEM((2 * ring, points, LANES), jnp.bfloat16),
            pltpu.VMEM((grid * pitch, LANES), jnp.float32),
            pltpu.VMEM((points, LANES), jnp.float32),
            pltpu.VMEM((points, LANES), jnp.float32),
            pltpu.VMEM((2, grid, grid, LANES), jnp.float32),
            pltpu.SemaphoreType.DMA((2 * ring,)),
            pltpu.SemaphoreType.DMA((4 + 2 * ring,)),
        ],
        compiler_params=pltpu.CompilerParams(collective_id=0, has_side_effects=True),
    )(*args)
    result = jnp.stack([total[:, :grid], total[:, HALF : HALF + grid]])
    return result.reshape(1, 2, 1, grid, points)


def solution(mesh):
    in_specs = (P("kpool", None, "band", None, None), P())
    out_specs = P("kpool", None, "band", None, None)
    return jax.shard_map(per_device, mesh=mesh, in_specs=in_specs, out_specs=out_specs, check_vma=False)
```

```python
import functools
import math

import jax
import jax.numpy as jnp
import numpy as np
from jax import lax
from jax.experimental import pallas as pl
from jax.experimental.pallas import tpu as pltpu
from jax.sharding import PartitionSpec as P

KMESH = 4
ROUNDS = 1
LANES = 128
HALF = 64
PITCH = 8
FAR = 1e30
BATCH = 48
MESH = pl.DeviceIdType.MESH


def kpoint_coords(label):
    digits = (label % KMESH, label // KMESH % KMESH, label // (KMESH * KMESH))
    return [digit.astype(jnp.float32) / KMESH for digit in digits]


def two_parts(table):
    high = table.astype(jnp.bfloat16)
    low = (table - high.astype(np.float32)).astype(jnp.bfloat16)
    return high, low


def dft_tables(grid):
    index = np.arange(grid)
    angles = (index[:, None] * index[None, :] % grid) * (2.0 * math.pi / grid)
    cosine = np.cos(angles).astype(np.float32)
    sine = np.sin(angles).astype(np.float32)
    lanes = []
    for sign in (1.0, -1.0):
        full = np.zeros((LANES, LANES), np.float32)
        full[:grid, :grid] = cosine
        full[HALF : HALF + grid, HALF : HALF + grid] = cosine
        full[:grid, HALF : HALF + grid] = -sign * sine
        full[HALF : HALF + grid, :grid] = sign * sine
        high, low = two_parts(full)
        lanes.append(np.block([[high, low], [high, np.zeros_like(low)]]))
    high, low = two_parts(np.concatenate([cosine, sine], axis=0))
    rows = np.concatenate([high, high, low], axis=1)
    return np.stack(lanes), rows


def split(x):
    high = x.astype(jnp.bfloat16)
    low = (x - high.astype(jnp.float32)).astype(jnp.bfloat16)
    return high, low


def visits(ring, n):
    return [n] + sorted((m for m in range(ring) if m != n), key=lambda m: (abs(m - n), (m - n) % 2 * 0 + (m ^ 1 != n)))


def squares(offset, grid, index):
    freq = jnp.where(index < grid // 2, index, index - grid).astype(jnp.float32)
    cut = (index == grid // 2) | (index >= grid)
    return jnp.where(cut, FAR, (offset + freq) ** 2)


def kernel(grid, ring, pools, pitch, batch, label_ref, sent_ref, lanes_ref, rows_ref, out_ref,
           bufs, field, band, a1_ref, a2_ref, acc1, acc2, v_ref, recv_sem, send_sem):
    me, n = lax.axis_index("kpool"), lax.axis_index("band")
    odd = me % 2
    turn = 1 - 2 * odd
    near = (me + turn + pools) % pools
    far = (me - turn + pools) % pools
    beyond = (me + 2 * turn + pools) % pools
    before = (me - 2 * turn + pools) % pools

    barrier = pltpu.get_barrier_semaphore()

    def hail(pool, band):
        pl.semaphore_signal(barrier, inc=1, device_id=(pool, band), device_id_type=MESH)

    for pool in (near, far, beyond, before):
        hail(pool, n)
    for plane in range(ring):
        @pl.when(n == plane)
        def _():
            count = 4
            for other in (plane - 1, plane + 1):
                if 0 <= other < ring:
                    hail(near, other)
                    hail(me, other)
                    count += 2
            pl.semaphore_wait(barrier, count)

    def place(plane, band, outer):
        return 2 * visits(ring, plane).index(band) + outer

    def copy(source, step, pool, band, slot):
        return pltpu.make_async_remote_copy(
            src_ref=source,
            dst_ref=bufs.at[step],
            send_sem=send_sem.at[slot],
            recv_sem=recv_sem.at[step],
            device_id=(pool, band),
            device_id_type=MESH,
        )

    def sends(plane):
        first = [(sent_ref, place(plane, plane, 0), near, plane, 0)]
        first.append((sent_ref, place(plane, plane, 1), far, plane, 1))
        slot = 2
        for other in (plane - 1, plane + 1):
            if 0 <= other < ring:
                first.append((sent_ref, place(other, plane, 0), near, other, slot))
                slot += 1
        later = {}
        for band in visits(ring, plane)[1:]:
            step = place(plane, band, 0)
            source = bufs.at[step]
            onward = plane + 1 if band < plane else plane - 1
            copies = []
            if 0 <= onward < ring:
                copies.append((source, place(onward, band, 0), me, onward, slot))
                slot += 1
            copies.append((source, place(plane, band, 1), beyond, plane, slot))
            slot += 1
            later[step] = copies
        return first, later

    def arrival(step):
        spot = bufs.at[step]
        pltpu.make_async_copy(spot, spot, recv_sem.at[step]).wait()

    def service(step, moment):
        for plane in range(ring):
            order = visits(ring, plane)
            due = []
            for at, band in enumerate(order):
                if at == 0:
                    continue
                when = 1 if abs(band - plane) == 1 else 2 * at - 1
                due.append((when, 2 * at))

            @pl.when(n == plane)
            def _():
                for when, number in due:
                    @pl.when(moment == when)
                    def _():
                        arrival(number)
                        for c in sends(plane)[1][number]:
                            copy(*c).start()

    for plane in range(ring):
        @pl.when(n == plane)
        def _():
            for c in sends(plane)[0]:
                copy(*c).start()

    lane = lax.broadcasted_iota(jnp.int32, (1, LANES), 1)
    sign = jnp.where(lane < HALF, 1.0, -1.0).astype(jnp.float32)
    scale = grid**1.5 / 16.0 / (grid * grid * grid)

    first = lane < HALF
    here = kpoint_coords(label_ref[me])
    column = lax.broadcasted_iota(jnp.int32, (grid, LANES), 0)
    for which, partner in enumerate((near, far)):
        there = kpoint_coords(label_ref[partner])
        off = [here[d] - there[d] for d in range(3)]
        plane_sum = squares(off[1], grid, column) + squares(off[2], grid, lane % HALF)

        def make_v(x, carry):
            shifted = (x - grid * (x // (grid // 2))).astype(jnp.float32) + off[0]
            edge = (x == grid // 2).astype(jnp.float32)
            total = plane_sum + (shifted * shifted + edge * FAR)
            v_ref[which, x] = jnp.where(total > 0.5 * FAR, 0.0, scale / total)
            return carry

        lax.fori_loop(0, grid, make_v, 0)

    def swap(x):
        return pltpu.roll(x, HALF, 1)

    def turned(x):
        return swap(x) * sign

    def tile(source, start):
        at, off = start // LANES, start % LANES
        halves = []
        for part in range(2):
            turn_by = (part * HALF - off) % LANES

            def lanes_of(column):
                x = source[part, :, column * LANES : (column + 1) * LANES].astype(jnp.float32)
                return pltpu.roll(x, turn_by, 1) if turn_by else x

            half = lanes_of(at)
            if off + grid > LANES:
                half = jnp.where(lane < part * HALF + LANES - off, half, lanes_of(at + 1))
            halves.append(half)
        return jnp.where(first, halves[0], halves[1])

    def along_lanes(x, which):
        high, low = split(x)
        out = jnp.dot(
            jnp.concatenate([high, low], axis=1), lanes_ref[which], preferred_element_type=jnp.float32
        )
        return out[:, :LANES] + out[:, LANES:]

    def along_rows(xs, sense):
        parts = []
        for x in xs:
            high, low = split(x)
            parts.append(jnp.concatenate([high, low, high], axis=0))
        outs = []
        for at in range(0, len(parts), 2):
            pair = jnp.concatenate(parts[at : at + 2], axis=1)
            out = jnp.dot(rows_ref[...], pair, preferred_element_type=jnp.float32)
            for j in range(len(parts[at : at + 2])):
                piece = out[:, j * LANES : (j + 1) * LANES]
                q = turned(piece[grid:])
                outs.append(piece[:grid] + q if sense > 0 else piece[:grid] - q)
        return outs

    def one_field(step, carry):
        @pl.when(step % 2 == 1)
        def _():
            service(step, step)

        @pl.when(jnp.logical_or(step == 0, step % 2 == 1))
        def _():
            arrival(step)

        which = step % 2
        source = bufs.at[step]

        for base in range(0, grid, batch):
            dens = []
            for y in range(base, base + batch):
                span = slice(y * grid, (y + 1) * grid)
                b = tile(source, y * grid)
                band[span, :] = b
                dens.append(b * a1_ref[span, :] + swap(b) * a2_ref[span, :])
            spec = along_lanes(jnp.concatenate(dens, axis=0), 0)
            outs = along_rows([spec[j * grid : (j + 1) * grid] for j in range(batch)], 1)
            for j in range(batch):
                field[(base + j) * pitch : (base + j) * pitch + grid, :] = outs[j]

        for base in range(0, grid, batch):
            xs = [field[pl.ds(base + j, grid, stride=pitch), :] for j in range(batch)]
            spec = along_rows(xs, 1)
            spec = [spec[j] * v_ref[which, base + j] for j in range(batch)]
            outs = along_rows(spec, -1)
            for j in range(batch):
                field[pl.ds(base + j, grid, stride=pitch), :] = outs[j]

        for base in range(0, grid, batch):
            mids = [field[(base + j) * pitch : (base + j) * pitch + grid, :] for j in range(batch)]
            outs = along_rows(mids, -1)
            pot = along_lanes(jnp.concatenate(outs, axis=0), 1)
            for j in range(batch):
                y = base + j
                span = slice(y * grid, (y + 1) * grid)
                b = band[span, :]
                piece = pot[j * grid : (j + 1) * grid]
                acc1[span, :] = acc1[span, :] + b * piece
                acc2[span, :] = acc2[span, :] + b * swap(piece)
        return carry

    group = math.lcm(grid, LANES)
    lines = group // grid

    def prepare(g, carry):
        view = sent_ref.at[:, :, pl.ds(pl.multiple_of(g * group, LANES), group)]
        for j in range(lines):
            a = tile(view, j * grid)
            other = swap(a)
            rows = pl.ds(pl.multiple_of((g * lines + j) * grid, 8), grid)
            a1_ref[rows, :] = jnp.where(first, a, -other)
            a2_ref[rows, :] = jnp.where(first, other, a)
        return carry

    lax.fori_loop(0, grid // lines, prepare, 0)
    acc1[...] = jnp.zeros_like(acc1)
    acc2[...] = jnp.zeros_like(acc2)
    lax.fori_loop(0, 2 * ring, one_field, 0)

    weight = -((2.0 * ROUNDS * ring) ** (-0.5))

    def finish(g, carry):
        made = [[None] * (group // LANES) for _ in range(2)]
        for j in range(lines):
            rows = pl.ds(pl.multiple_of((g * lines + j) * grid, 8), grid)
            one = acc1[rows, :]
            two = acc2[rows, :]
            start = j * grid
            at, off = start // LANES, start % LANES
            for part, value in enumerate((one - swap(one), two + swap(two))):
                value = pltpu.roll(value * weight, off, 1) if off else value * weight
                row = made[part]
                row[at] = value if off == 0 else jnp.where(lane < off, row[at], value)
                if off + grid > LANES:
                    row[at + 1] = value
        for part in range(2):
            for at in range(group // LANES):
                lanes_at = pl.ds(pl.multiple_of(g * group + at * LANES, LANES), LANES)
                out_ref[part, :, lanes_at] = made[part][at]
        return carry

    lax.fori_loop(0, grid // lines, finish, 0)

    for plane in range(ring):
        @pl.when(n == plane)
        def _():
            begun, later = sends(plane)
            for c in begun:
                copy(*c).wait_send()
            for copies in later.values():
                for c in copies:
                    copy(*c).wait_send()


def per_device(psi, kpoint_of_pool):
    own = psi[0, :, 0]
    grid, points = own.shape[1], own.shape[2]
    ring = lax.axis_size("band")
    pools = lax.axis_size("kpool")
    lanes, rows = dft_tables(grid)
    whole = pl.BlockSpec(memory_space=pltpu.VMEM)
    pitch = grid + PITCH
    total = pl.pallas_call(
        functools.partial(kernel, grid, ring, pools, pitch, BATCH),
        in_specs=[pl.BlockSpec(memory_space=pltpu.SMEM)] + [whole] * 3,
        out_specs=whole,
        out_shape=jax.ShapeDtypeStruct(own.shape, jnp.float32),
        scratch_shapes=[
            pltpu.VMEM((2 * ring,) + own.shape, jnp.bfloat16),
            pltpu.VMEM((grid * pitch, LANES), jnp.float32),
            pltpu.VMEM((points, LANES), jnp.float32),
            pltpu.VMEM((points, LANES), jnp.float32),
            pltpu.VMEM((points, LANES), jnp.float32),
            pltpu.VMEM((points, LANES), jnp.float32),
            pltpu.VMEM((points, LANES), jnp.float32),
            pltpu.VMEM((2, grid, grid, LANES), jnp.float32),
            pltpu.SemaphoreType.DMA((2 * ring,)),
            pltpu.SemaphoreType.DMA((4 + 2 * ring,)),
        ],
        compiler_params=pltpu.CompilerParams(collective_id=0, has_side_effects=True),
    )(kpoint_of_pool, own, jnp.asarray(lanes), jnp.asarray(rows))
    return total[None, :, None]


def solution(mesh):
    in_specs = (P("kpool", None, "band", None, None), P())
    out_specs = P("kpool", None, "band", None, None)
    return jax.shard_map(per_device, mesh=mesh, in_specs=in_specs, out_specs=out_specs, check_vma=False)
```

```python
import functools
import math

import jax
import jax.numpy as jnp
import numpy as np
from jax import lax
from jax.experimental import pallas as pl
from jax.experimental.pallas import tpu as pltpu
from jax.sharding import PartitionSpec as P

KMESH = 4
ROUNDS = 1
LANES = 128
HALF = 64
PITCH = 8
FAR = 1e30
BATCH = 48
MESH = pl.DeviceIdType.MESH


def kpoint_coords(label):
    digits = (label % KMESH, label // KMESH % KMESH, label // (KMESH * KMESH))
    return [digit.astype(jnp.float32) / KMESH for digit in digits]


def two_parts(table):
    high = table.astype(jnp.bfloat16)
    low = (table - high.astype(np.float32)).astype(jnp.bfloat16)
    return high, low


def dft_tables(grid):
    index = np.arange(grid)
    angles = (index[:, None] * index[None, :] % grid) * (2.0 * math.pi / grid)
    cosine = np.cos(angles).astype(np.float32)
    sine = np.sin(angles).astype(np.float32)
    lanes = []
    for sign in (1.0, -1.0):
        full = np.zeros((LANES, LANES), np.float32)
        full[:grid, :grid] = cosine
        full[HALF : HALF + grid, HALF : HALF + grid] = cosine
        full[:grid, HALF : HALF + grid] = -sign * sine
        full[HALF : HALF + grid, :grid] = sign * sine
        high, low = two_parts(full)
        lanes.append(np.block([[high, low], [high, np.zeros_like(low)]]))
    high, low = two_parts(np.concatenate([cosine, sine], axis=0))
    rows = np.concatenate([high, high, low], axis=1)
    return np.stack(lanes), rows


def split(x):
    high = x.astype(jnp.bfloat16)
    low = (x - high.astype(jnp.float32)).astype(jnp.bfloat16)
    return high, low


def visits(ring, n):
    return [n] + sorted((m for m in range(ring) if m != n), key=lambda m: (abs(m - n), (m - n) % 2 * 0 + (m ^ 1 != n)))


def squares(offset, grid, index):
    freq = jnp.where(index < grid // 2, index, index - grid).astype(jnp.float32)
    cut = (index == grid // 2) | (index >= grid)
    return jnp.where(cut, FAR, (offset + freq) ** 2)


def kernel(grid, ring, pools, pitch, batch, label_ref, sent_ref, lanes_ref, rows_ref, out_ref,
           bufs, field, band, a1_ref, a2_ref, acc1, acc2, v_ref, recv_sem, send_sem):
    me, n = lax.axis_index("kpool"), lax.axis_index("band")
    odd = me % 2
    turn = 1 - 2 * odd
    near = (me + turn + pools) % pools
    far = (me - turn + pools) % pools
    beyond = (me + 2 * turn + pools) % pools
    before = (me - 2 * turn + pools) % pools

    barrier = pltpu.get_barrier_semaphore()

    def hail(pool, band):
        pl.semaphore_signal(barrier, inc=1, device_id=(pool, band), device_id_type=MESH)

    for pool in (near, far, beyond, before):
        hail(pool, n)
    for plane in range(ring):
        @pl.when(n == plane)
        def _():
            count = 4
            for other in (plane - 1, plane + 1):
                if 0 <= other < ring:
                    hail(near, other)
                    hail(me, other)
                    count += 2
            pl.semaphore_wait(barrier, count)

    def place(plane, band, outer):
        return 2 * visits(ring, plane).index(band) + outer

    def copy(half, source, step, pool, band, slot):
        return pltpu.make_async_remote_copy(
            src_ref=source.at[half],
            dst_ref=bufs.at[step, half],
            send_sem=send_sem.at[slot, half],
            recv_sem=recv_sem.at[step, half],
            device_id=(pool, band),
            device_id_type=MESH,
        )

    def sends(plane):
        first = [(sent_ref, place(plane, plane, 0), near, plane, 0)]
        first.append((sent_ref, place(plane, plane, 1), far, plane, 1))
        slot = 2
        for other in (plane - 1, plane + 1):
            if 0 <= other < ring:
                first.append((sent_ref, place(other, plane, 0), near, other, slot))
                slot += 1
        later = {}
        for band in visits(ring, plane)[1:]:
            step = place(plane, band, 0)
            source = bufs.at[step]
            onward = plane + 1 if band < plane else plane - 1
            copies = []
            if 0 <= onward < ring:
                copies.append((source, place(onward, band, 0), me, onward, slot))
                slot += 1
            copies.append((source, place(plane, band, 1), beyond, plane, slot))
            slot += 1
            later[step] = copies
        return first, later

    def arrival(step, half):
        spot = bufs.at[step, half]
        pltpu.make_async_copy(spot, spot, recv_sem.at[step, half]).wait()

    def moments(distance):
        if distance == 1:
            return (2, 2)
        return (4 * distance - 3, 4 * distance - 2)

    def service(moment, odd_moments):
        for plane in range(ring):
            due = {}
            for at, band in enumerate(visits(ring, plane)):
                if at > 0:
                    for half, when in enumerate(moments(abs(band - plane))):
                        if when % 2 == odd_moments:
                            due.setdefault(when, []).append((2 * at, half))

            @pl.when(n == plane)
            def _():
                for when, events in due.items():
                    @pl.when(moment == when)
                    def _():
                        for number, half in sorted(events, key=lambda e: e[1]):
                            arrival(number, half)
                            for c in sends(plane)[1][number]:
                                copy(half, *c).start()

    for plane in range(ring):
        @pl.when(n == plane)
        def _():
            for c in sends(plane)[0]:
                for half in range(2):
                    copy(half, *c).start()

    lane = lax.broadcasted_iota(jnp.int32, (1, LANES), 1)
    sign = jnp.where(lane < HALF, 1.0, -1.0).astype(jnp.float32)
    scale = grid**1.5 / 16.0 / (grid * grid * grid)

    first = lane < HALF
    here = kpoint_coords(label_ref[me])
    column = lax.broadcasted_iota(jnp.int32, (grid, LANES), 0)
    for which, partner in enumerate((near, far)):
        there = kpoint_coords(label_ref[partner])
        off = [here[d] - there[d] for d in range(3)]
        plane_sum = squares(off[1], grid, column) + squares(off[2], grid, lane % HALF)

        def make_v(x, carry):
            shifted = (x - grid * (x // (grid // 2))).astype(jnp.float32) + off[0]
            edge = (x == grid // 2).astype(jnp.float32)
            total = plane_sum + (shifted * shifted + edge * FAR)
            v_ref[which, x] = jnp.where(total > 0.5 * FAR, 0.0, scale / total)
            return carry

        lax.fori_loop(0, grid, make_v, 0)

    def swap(x):
        return pltpu.roll(x, HALF, 1)

    def turned(x):
        return swap(x) * sign

    def tile(source, start):
        at, off = start // LANES, start % LANES
        halves = []
        for part in range(2):
            turn_by = (part * HALF - off) % LANES

            def lanes_of(column):
                x = source[part, :, column * LANES : (column + 1) * LANES].astype(jnp.float32)
                return pltpu.roll(x, turn_by, 1) if turn_by else x

            half = lanes_of(at)
            if off + grid > LANES:
                half = jnp.where(lane < part * HALF + LANES - off, half, lanes_of(at + 1))
            halves.append(half)
        return jnp.where(first, halves[0], halves[1])

    def along_lanes(x, which):
        high, low = split(x)
        out = jnp.dot(
            jnp.concatenate([high, low], axis=1), lanes_ref[which], preferred_element_type=jnp.float32
        )
        return out[:, :LANES] + out[:, LANES:]

    def along_rows(xs, sense):
        parts = []
        for x in xs:
            high, low = split(x)
            parts.append(jnp.concatenate([high, low, high], axis=0))
        outs = []
        for at in range(0, len(parts), 2):
            pair = jnp.concatenate(parts[at : at + 2], axis=1)
            out = jnp.dot(rows_ref[...], pair, preferred_element_type=jnp.float32)
            for j in range(len(parts[at : at + 2])):
                piece = out[:, j * LANES : (j + 1) * LANES]
                q = turned(piece[grid:])
                outs.append(piece[:grid] + q if sense > 0 else piece[:grid] - q)
        return outs

    def one_field(step, carry):
        @pl.when(step % 2 == 1)
        def _():
            service(2 * step, 0)

        @pl.when(jnp.logical_or(step == 0, step % 2 == 1))
        def _():
            for half in range(2):
                arrival(step, half)

        which = step % 2
        source = bufs.at[step]

        for base in range(0, grid, batch):
            dens = []
            for y in range(base, base + batch):
                span = slice(y * grid, (y + 1) * grid)
                b = tile(source, y * grid)
                band[span, :] = b
                dens.append(b * a1_ref[span, :] + swap(b) * a2_ref[span, :])
            spec = along_lanes(jnp.concatenate(dens, axis=0), 0)
            outs = along_rows([spec[j * grid : (j + 1) * grid] for j in range(batch)], 1)
            for j in range(batch):
                field[(base + j) * pitch : (base + j) * pitch + grid, :] = outs[j]

        @pl.when(step % 2 == 0)
        def _():
            service(2 * step + 1, 1)

        for base in range(0, grid, batch):
            xs = [field[pl.ds(base + j, grid, stride=pitch), :] for j in range(batch)]
            spec = along_rows(xs, 1)
            spec = [spec[j] * v_ref[which, base + j] for j in range(batch)]
            outs = along_rows(spec, -1)
            for j in range(batch):
                field[pl.ds(base + j, grid, stride=pitch), :] = outs[j]

        for base in range(0, grid, batch):
            mids = [field[(base + j) * pitch : (base + j) * pitch + grid, :] for j in range(batch)]
            outs = along_rows(mids, -1)
            pot = along_lanes(jnp.concatenate(outs, axis=0), 1)
            for j in range(batch):
                y = base + j
                span = slice(y * grid, (y + 1) * grid)
                b = band[span, :]
                piece = pot[j * grid : (j + 1) * grid]
                acc1[span, :] = acc1[span, :] + b * piece
                acc2[span, :] = acc2[span, :] + b * swap(piece)
        return carry

    group = math.lcm(grid, LANES)
    lines = group // grid

    def prepare(g, carry):
        view = sent_ref.at[:, :, pl.ds(pl.multiple_of(g * group, LANES), group)]
        for j in range(lines):
            a = tile(view, j * grid)
            other = swap(a)
            rows = pl.ds(pl.multiple_of((g * lines + j) * grid, 8), grid)
            a1_ref[rows, :] = jnp.where(first, a, -other)
            a2_ref[rows, :] = jnp.where(first, other, a)
        return carry

    lax.fori_loop(0, grid // lines, prepare, 0)
    acc1[...] = jnp.zeros_like(acc1)
    acc2[...] = jnp.zeros_like(acc2)
    lax.fori_loop(0, 2 * ring, one_field, 0)

    def finish(g, carry):
        made = [[None] * (group // LANES) for _ in range(2)]
        for j in range(lines):
            rows = pl.ds(pl.multiple_of((g * lines + j) * grid, 8), grid)
            one = acc1[rows, :]
            two = acc2[rows, :]
            start = j * grid
            at, off = start // LANES, start % LANES
            for part, value in enumerate((one - swap(one), two + swap(two))):
                value = pltpu.roll(value, off, 1) if off else value
                row = made[part]
                row[at] = value if off == 0 else jnp.where(lane < off, row[at], value)
                if off + grid > LANES:
                    row[at + 1] = value
        for part in range(2):
            for at in range(group // LANES):
                lanes_at = pl.ds(pl.multiple_of(g * group + at * LANES, LANES), LANES)
                out_ref[part, :, lanes_at] = made[part][at]
        return carry

    lax.fori_loop(0, grid // lines, finish, 0)

    for plane in range(ring):
        @pl.when(n == plane)
        def _():
            begun, later = sends(plane)
            for copies in [begun, *later.values()]:
                for c in copies:
                    for half in range(2):
                        copy(half, *c).wait_send()


def per_device(psi, kpoint_of_pool):
    own, own_bands = psi[0, :, 0], psi.shape[2]
    grid, points = own.shape[1], own.shape[2]
    ring = lax.axis_size("band")
    pools = lax.axis_size("kpool")
    lanes, rows = dft_tables(grid)
    whole = pl.BlockSpec(memory_space=pltpu.VMEM)
    pitch = grid + PITCH
    total = pl.pallas_call(
        functools.partial(kernel, grid, ring, pools, pitch, BATCH),
        in_specs=[pl.BlockSpec(memory_space=pltpu.SMEM)] + [whole] * 3,
        out_specs=whole,
        out_shape=jax.ShapeDtypeStruct(own.shape, jnp.float32),
        scratch_shapes=[
            pltpu.VMEM((2 * ring,) + own.shape, jnp.bfloat16),
            pltpu.VMEM((grid * pitch, LANES), jnp.float32),
            pltpu.VMEM((points, LANES), jnp.float32),
            pltpu.VMEM((points, LANES), jnp.float32),
            pltpu.VMEM((points, LANES), jnp.float32),
            pltpu.VMEM((points, LANES), jnp.float32),
            pltpu.VMEM((points, LANES), jnp.float32),
            pltpu.VMEM((2, grid, grid, LANES), jnp.float32),
            pltpu.SemaphoreType.DMA((2 * ring, 2)),
            pltpu.SemaphoreType.DMA((4 + 2 * ring, 2)),
        ],
        compiler_params=pltpu.CompilerParams(collective_id=0, has_side_effects=True),
    )(kpoint_of_pool, own, jnp.asarray(lanes), jnp.asarray(rows))
    weight = -((2.0 * ROUNDS * ring * own_bands) ** (-0.5))
    return (total * weight)[None, :, None]


def solution(mesh):
    in_specs = (P("kpool", None, "band", None, None), P())
    out_specs = P("kpool", None, "band", None, None)
    return jax.shard_map(per_device, mesh=mesh, in_specs=in_specs, out_specs=out_specs, check_vma=False)
```

```python
import functools
import math

import jax
import jax.numpy as jnp
import numpy as np
from jax import lax
from jax.experimental import pallas as pl
from jax.experimental.pallas import tpu as pltpu
from jax.sharding import PartitionSpec as P

KMESH = 4
ROUNDS = 1
LANES = 128
HALF = 64
PITCH = 8
FAR = 1e30
BATCH = 48
MESH = pl.DeviceIdType.MESH


def kpoint_coords(label):
    digits = (label % KMESH, label // KMESH % KMESH, label // (KMESH * KMESH))
    return [digit.astype(jnp.float32) / KMESH for digit in digits]


def two_parts(table):
    high = table.astype(jnp.bfloat16)
    low = (table - high.astype(np.float32)).astype(jnp.bfloat16)
    return high, low


def dft_tables(grid):
    index = np.arange(grid)
    angles = (index[:, None] * index[None, :] % grid) * (2.0 * math.pi / grid)
    cosine = np.cos(angles).astype(np.float32)
    sine = np.sin(angles).astype(np.float32)
    lanes = []
    for sign in (1.0, -1.0):
        full = np.zeros((LANES, LANES), np.float32)
        full[:grid, :grid] = cosine
        full[HALF : HALF + grid, HALF : HALF + grid] = cosine
        full[:grid, HALF : HALF + grid] = -sign * sine
        full[HALF : HALF + grid, :grid] = sign * sine
        high, low = two_parts(full)
        lanes.append(np.block([[high, low], [high, np.zeros_like(low)]]))
    high, low = two_parts(np.concatenate([cosine, sine], axis=0))
    rows = np.concatenate([high, high, low], axis=1)
    return np.stack(lanes), rows


def split(x):
    high = x.astype(jnp.bfloat16)
    low = (x - high.astype(jnp.float32)).astype(jnp.bfloat16)
    return high, low


def over_z(ring, plane, band, parity):
    if 0 < plane < ring - 1:
        return abs(band - plane) == 1
    return parity == 0 and abs(band - plane) == ring - 1 > 1


def visits(ring, plane):
    inner = 0 < plane < ring - 1
    others = sorted((m for m in range(ring) if m != plane), key=lambda m: (abs(m - plane), m ^ 1 != plane))
    order = [(0, plane), (1, plane)]
    if not inner:
        for band in others:
            order += [(0, band), (1, band)]
        return order
    close = [m for m in others if abs(m - plane) == 1]
    distant = [m for m in others if abs(m - plane) > 1]
    order += [(0, m) for m in close] + [(1, close[0])]
    for band in distant:
        order += [(0, band), (1, band)]
    return order + [(1, m) for m in close[1:]]


def forwards(ring, plane, parity, kind, band):
    found = []
    if kind == 0 and band != plane:
        onward = plane + 1 if band < plane else plane - 1
        if 0 <= onward < ring:
            found.append((0, "me", onward))
        if not over_z(ring, plane, band, parity):
            found.append((1, "beyond", plane))
    if kind == 1:
        for onward in (plane - 1, plane + 1):
            if 0 <= onward < ring and (band - plane) * (plane - onward) >= 0:
                if over_z(ring, onward, band, parity):
                    found.append((1, "me", onward))
    return found


def moments(ring, plane, parity):
    inner = 0 < plane < ring - 1
    table = {}
    for step, (kind, band) in enumerate(visits(ring, plane)):
        distance = abs(band - plane)
        when = (2 * step, 2 * step)
        sends = forwards(ring, plane, parity, kind, band)
        if sends and kind == 0:
            if distance == 1:
                when = (1, 2)
            elif distance == 2:
                when = (5, 7) if inner else (5, 6)
            else:
                when = (4 * distance - 3, 4 * distance - 2)
        elif sends and distance > 0:
            when = (2 * step - 3, 2 * step - 1)
        for half in range(2):
            assert when[half] <= 2 * step
            table.setdefault(when[half], []).append((kind, half, step, sends, band))
    return {when: sorted(events, key=lambda e: e[:3]) for when, events in table.items()}


def squares(offset, grid, index):
    freq = jnp.where(index < grid // 2, index, index - grid).astype(jnp.float32)
    cut = (index == grid // 2) | (index >= grid)
    return jnp.where(cut, FAR, (offset + freq) ** 2)


def kernel(grid, ring, pools, pitch, batch, label_ref, sent_ref, lanes_ref, rows_ref, out_ref,
           bufs, field, band, a1_ref, a2_ref, acc1, acc2, v_ref, recv_sem, send_sem):
    me, n = lax.axis_index("kpool"), lax.axis_index("band")
    odd = me % 2
    turn = 1 - 2 * odd
    near = (me + turn + pools) % pools
    far = (me - turn + pools) % pools
    beyond = (me + 2 * turn + pools) % pools
    before = (me - 2 * turn + pools) % pools

    barrier = pltpu.get_barrier_semaphore()

    def hail(pool, band):
        pl.semaphore_signal(barrier, inc=1, device_id=(pool, band), device_id_type=MESH)

    for pool in (near, far, beyond, before):
        hail(pool, n)
    for plane in range(ring):
        @pl.when(n == plane)
        def _():
            count = 4
            for other in (plane - 1, plane + 1):
                if 0 <= other < ring:
                    hail(near, other)
                    hail(me, other)
                    count += 2
            pl.semaphore_wait(barrier, count)

    def place(plane, band, kind):
        return visits(ring, plane).index((kind, band))

    def copy(half, source, step, pool, band, slot):
        return pltpu.make_async_remote_copy(
            src_ref=source.at[half],
            dst_ref=bufs.at[step, half],
            send_sem=send_sem.at[slot, half],
            recv_sem=recv_sem.at[step, half],
            device_id=(pool, band),
            device_id_type=MESH,
        )

    def own_sends(plane):
        found = [
            (sent_ref, place(plane, plane, 0), near, plane, 0),
            (sent_ref, place(plane, plane, 1), far, plane, 1),
        ]
        for other in (plane - 1, plane + 1):
            if 0 <= other < ring:
                found.append((sent_ref, place(other, plane, 0), near, other, len(found)))
        return found

    def later_sends(plane, parity):
        found, slot = {}, 4
        for step, (kind, band) in enumerate(visits(ring, plane)):
            found[step] = []
            for to_kind, pool, onward in forwards(ring, plane, parity, kind, band):
                target = me if pool == "me" else beyond
                found[step].append((bufs.at[step], place(onward, band, to_kind), target, onward, slot))
                slot += 1
        return found

    def classes(act):
        for plane in range(ring):
            for parity in range(2):
                pl.when(jnp.logical_and(n == plane, odd == parity))(functools.partial(act, plane, parity))

    def service(step, middle):
        def act(plane, parity):
            for when, events in moments(ring, plane, parity).items():
                if when % 2 == middle:

                    @pl.when(step == when // 2)
                    def _():
                        for kind, half, number, sends, band in events:
                            spot = bufs.at[number, half]
                            pltpu.make_async_copy(spot, spot, recv_sem.at[number, half]).wait()
                            for c in later_sends(plane, parity)[number]:
                                copy(half, *c).start()

        classes(act)

    def begin(plane, parity):
        for c in own_sends(plane):
            for half in range(2):
                copy(half, *c).start()

    classes(begin)

    lists = 0
    for plane in range(ring):
        bits = sum(kind << step for step, (kind, _) in enumerate(visits(ring, plane)))
        lists = lists + (n == plane).astype(jnp.int32) * bits

    lane = lax.broadcasted_iota(jnp.int32, (1, LANES), 1)
    sign = jnp.where(lane < HALF, 1.0, -1.0).astype(jnp.float32)
    scale = grid**1.5 / 16.0 / (grid * grid * grid)

    first = lane < HALF
    here = kpoint_coords(label_ref[me])
    column = lax.broadcasted_iota(jnp.int32, (grid, LANES), 0)
    for which, partner in enumerate((near, far)):
        there = kpoint_coords(label_ref[partner])
        off = [here[d] - there[d] for d in range(3)]
        plane_sum = squares(off[1], grid, column) + squares(off[2], grid, lane % HALF)

        def make_v(x, carry):
            shifted = (x - grid * (x // (grid // 2))).astype(jnp.float32) + off[0]
            edge = (x == grid // 2).astype(jnp.float32)
            total = plane_sum + (shifted * shifted + edge * FAR)
            v_ref[which, x] = jnp.where(total > 0.5 * FAR, 0.0, scale / total)
            return carry

        lax.fori_loop(0, grid, make_v, 0)

    def swap(x):
        return pltpu.roll(x, HALF, 1)

    def turned(x):
        return swap(x) * sign

    def tile(source, start):
        at, off = start // LANES, start % LANES
        halves = []
        for part in range(2):
            turn_by = (part * HALF - off) % LANES

            def lanes_of(column):
                x = source[part, :, column * LANES : (column + 1) * LANES].astype(jnp.float32)
                return pltpu.roll(x, turn_by, 1) if turn_by else x

            half = lanes_of(at)
            if off + grid > LANES:
                half = jnp.where(lane < part * HALF + LANES - off, half, lanes_of(at + 1))
            halves.append(half)
        return jnp.where(first, halves[0], halves[1])

    def along_lanes(x, which):
        high, low = split(x)
        out = jnp.dot(
            jnp.concatenate([high, low], axis=1), lanes_ref[which], preferred_element_type=jnp.float32
        )
        return out[:, :LANES] + out[:, LANES:]

    def along_rows(xs, sense):
        parts = []
        for x in xs:
            high, low = split(x)
            parts.append(jnp.concatenate([high, low, high], axis=0))
        outs = []
        for at in range(0, len(parts), 2):
            pair = jnp.concatenate(parts[at : at + 2], axis=1)
            out = jnp.dot(rows_ref[...], pair, preferred_element_type=jnp.float32)
            for j in range(len(parts[at : at + 2])):
                piece = out[:, j * LANES : (j + 1) * LANES]
                q = turned(piece[grid:])
                outs.append(piece[:grid] + q if sense > 0 else piece[:grid] - q)
        return outs

    def one_field(step, carry):
        service(step, 0)
        which = jnp.right_shift(lists, step) % 2
        source = bufs.at[step]

        for base in range(0, grid, batch):
            dens = []
            for y in range(base, base + batch):
                span = slice(y * grid, (y + 1) * grid)
                b = tile(source, y * grid)
                band[span, :] = b
                dens.append(b * a1_ref[span, :] + swap(b) * a2_ref[span, :])
            spec = along_lanes(jnp.concatenate(dens, axis=0), 0)
            outs = along_rows([spec[j * grid : (j + 1) * grid] for j in range(batch)], 1)
            for j in range(batch):
                field[(base + j) * pitch : (base + j) * pitch + grid, :] = outs[j]

        service(step, 1)

        for base in range(0, grid, batch):
            xs = [field[pl.ds(base + j, grid, stride=pitch), :] for j in range(batch)]
            spec = along_rows(xs, 1)
            spec = [spec[j] * v_ref[which, base + j] for j in range(batch)]
            outs = along_rows(spec, -1)
            for j in range(batch):
                field[pl.ds(base + j, grid, stride=pitch), :] = outs[j]

        for base in range(0, grid, batch):
            mids = [field[(base + j) * pitch : (base + j) * pitch + grid, :] for j in range(batch)]
            outs = along_rows(mids, -1)
            pot = along_lanes(jnp.concatenate(outs, axis=0), 1)
            for j in range(batch):
                y = base + j
                span = slice(y * grid, (y + 1) * grid)
                b = band[span, :]
                piece = pot[j * grid : (j + 1) * grid]
                acc1[span, :] = acc1[span, :] + b * piece
                acc2[span, :] = acc2[span, :] + b * swap(piece)
        return carry

    group = math.lcm(grid, LANES)
    lines = group // grid

    def prepare(g, carry):
        view = sent_ref.at[:, :, pl.ds(pl.multiple_of(g * group, LANES), group)]
        for j in range(lines):
            a = tile(view, j * grid)
            other = swap(a)
            rows = pl.ds(pl.multiple_of((g * lines + j) * grid, 8), grid)
            a1_ref[rows, :] = jnp.where(first, a, -other)
            a2_ref[rows, :] = jnp.where(first, other, a)
        return carry

    lax.fori_loop(0, grid // lines, prepare, 0)
    acc1[...] = jnp.zeros_like(acc1)
    acc2[...] = jnp.zeros_like(acc2)
    lax.fori_loop(0, 2 * ring, one_field, 0)

    def finish(g, carry):
        made = [[None] * (group // LANES) for _ in range(2)]
        for j in range(lines):
            rows = pl.ds(pl.multiple_of((g * lines + j) * grid, 8), grid)
            one = acc1[rows, :]
            two = acc2[rows, :]
            start = j * grid
            at, off = start // LANES, start % LANES
            for part, value in enumerate((one - swap(one), two + swap(two))):
                value = pltpu.roll(value, off, 1) if off else value
                row = made[part]
                row[at] = value if off == 0 else jnp.where(lane < off, row[at], value)
                if off + grid > LANES:
                    row[at + 1] = value
        for part in range(2):
            for at in range(group // LANES):
                lanes_at = pl.ds(pl.multiple_of(g * group + at * LANES, LANES), LANES)
                out_ref[part, :, lanes_at] = made[part][at]
        return carry

    lax.fori_loop(0, grid // lines, finish, 0)

    def settle(plane, parity):
        for copies in [own_sends(plane), *later_sends(plane, parity).values()]:
            for c in copies:
                for half in range(2):
                    copy(half, *c).wait_send()

    classes(settle)


def per_device(psi, kpoint_of_pool):
    own, own_bands = psi[0, :, 0], psi.shape[2]
    grid, points = own.shape[1], own.shape[2]
    ring = lax.axis_size("band")
    pools = lax.axis_size("kpool")
    lanes, rows = dft_tables(grid)
    whole = pl.BlockSpec(memory_space=pltpu.VMEM)
    pitch = grid + PITCH
    total = pl.pallas_call(
        functools.partial(kernel, grid, ring, pools, pitch, BATCH),
        in_specs=[pl.BlockSpec(memory_space=pltpu.SMEM)] + [whole] * 3,
        out_specs=whole,
        out_shape=pltpu.VMEM(own.shape, jnp.float32),
        scratch_shapes=[
            pltpu.VMEM((2 * ring,) + own.shape, jnp.bfloat16),
            pltpu.VMEM((grid * pitch, LANES), jnp.float32),
            pltpu.VMEM((points, LANES), jnp.float32),
            pltpu.VMEM((points, LANES), jnp.float32),
            pltpu.VMEM((points, LANES), jnp.float32),
            pltpu.VMEM((points, LANES), jnp.float32),
            pltpu.VMEM((points, LANES), jnp.float32),
            pltpu.VMEM((2, grid, grid, LANES), jnp.float32),
            pltpu.SemaphoreType.DMA((2 * ring, 2)),
            pltpu.SemaphoreType.DMA((4 + 3 * ring, 2)),
        ],
        compiler_params=pltpu.CompilerParams(collective_id=0, has_side_effects=True),
    )(kpoint_of_pool, own, jnp.asarray(lanes), jnp.asarray(rows))
    weight = -((2.0 * ROUNDS * ring * own_bands) ** (-0.5))
    return (total * weight)[None, :, None]


def solution(mesh):
    in_specs = (P("kpool", None, "band", None, None), P())
    out_specs = P("kpool", None, "band", None, None)
    return jax.shard_map(per_device, mesh=mesh, in_specs=in_specs, out_specs=out_specs, check_vma=False)
```

```python
import functools
import math

import jax
import jax.numpy as jnp
import numpy as np
from jax import lax
from jax.experimental import pallas as pl
from jax.experimental.pallas import tpu as pltpu
from jax.sharding import PartitionSpec as P

KMESH = 4
ROUNDS = 1
LANES = 128
HALF = 64
PITCH = 8
FAR = 1e30
BATCH = 48
MESH = pl.DeviceIdType.MESH


def kpoint_coords(label):
    digits = (label % KMESH, label // KMESH % KMESH, label // (KMESH * KMESH))
    return [digit.astype(jnp.float32) / KMESH for digit in digits]


def two_parts(table):
    high = table.astype(jnp.bfloat16)
    low = (table - high.astype(np.float32)).astype(jnp.bfloat16)
    return high, low


def dft_tables(grid):
    index = np.arange(grid)
    angles = (index[:, None] * index[None, :] % grid) * (2.0 * math.pi / grid)
    cosine = np.cos(angles).astype(np.float32)
    sine = np.sin(angles).astype(np.float32)
    lanes = []
    for sign in (1.0, -1.0):
        full = np.zeros((LANES, LANES), np.float32)
        full[:grid, :grid] = cosine
        full[HALF : HALF + grid, HALF : HALF + grid] = cosine
        full[:grid, HALF : HALF + grid] = -sign * sine
        full[HALF : HALF + grid, :grid] = sign * sine
        high, low = two_parts(full)
        lanes.append(np.block([[high, low], [high, np.zeros_like(low)]]))
    high, low = two_parts(np.concatenate([cosine, sine], axis=0))
    rows = np.concatenate([high, high, low], axis=1)
    return np.stack(lanes), rows


def split(x):
    high = x.astype(jnp.bfloat16)
    low = (x - high.astype(jnp.float32)).astype(jnp.bfloat16)
    return high, low


def over_z(ring, plane, band, parity):
    if 0 < plane < ring - 1:
        return abs(band - plane) == 1
    return parity == 0 and abs(band - plane) == ring - 1 > 1


def visits(ring, plane):
    inner = 0 < plane < ring - 1
    others = sorted((m for m in range(ring) if m != plane), key=lambda m: (abs(m - plane), m ^ 1 != plane))
    order = [(0, plane), (1, plane)]
    if not inner:
        for band in others:
            order += [(0, band), (1, band)]
        return order
    close = [m for m in others if abs(m - plane) == 1]
    distant = [m for m in others if abs(m - plane) > 1]
    order += [(0, m) for m in close] + [(1, close[0])]
    for band in distant:
        order += [(0, band), (1, band)]
    return order + [(1, m) for m in close[1:]]


def forwards(ring, plane, parity, kind, band):
    found = []
    if kind == 0 and band != plane:
        onward = plane + 1 if band < plane else plane - 1
        if 0 <= onward < ring:
            found.append((0, "me", onward))
        if not over_z(ring, plane, band, parity):
            found.append((1, "beyond", plane))
    if kind == 1:
        for onward in (plane - 1, plane + 1):
            if 0 <= onward < ring and (band - plane) * (plane - onward) >= 0:
                if over_z(ring, onward, band, parity):
                    found.append((1, "me", onward))
    return found


def moments(ring, plane, parity):
    inner = 0 < plane < ring - 1
    table = {}
    for step, (kind, band) in enumerate(visits(ring, plane)):
        distance = abs(band - plane)
        when = (2 * step, 2 * step)
        sends = forwards(ring, plane, parity, kind, band)
        if sends and kind == 0:
            if distance == 1:
                when = (1, 2)
            elif distance == 2:
                when = (5, 7) if inner else (5, 6)
            else:
                when = (4 * distance - 3, 4 * distance - 2)
        elif sends and distance > 0:
            when = (2 * step - 3, 2 * step - 1)
        when = tuple(min(w + w % 2, 2 * step) for w in when)
        for half in range(2):
            assert when[half] <= 2 * step
            table.setdefault(when[half], []).append((kind, half, step, sends, band))
    return {when: sorted(events, key=lambda e: e[:3]) for when, events in table.items()}


def squares(offset, grid, index):
    freq = jnp.where(index < grid // 2, index, index - grid).astype(jnp.float32)
    cut = (index == grid // 2) | (index >= grid)
    return jnp.where(cut, FAR, (offset + freq) ** 2)


def kernel(grid, ring, pools, pitch, batch, label_ref, sent_ref, lanes_ref, rows_ref, out_ref,
           bufs, field, band, a1_ref, a2_ref, acc1, acc2, v_ref, recv_sem, send_sem):
    me, n = lax.axis_index("kpool"), lax.axis_index("band")
    odd = me % 2
    turn = 1 - 2 * odd
    near = (me + turn + pools) % pools
    far = (me - turn + pools) % pools
    beyond = (me + 2 * turn + pools) % pools
    before = (me - 2 * turn + pools) % pools

    barrier = pltpu.get_barrier_semaphore()

    def hail(pool, band):
        pl.semaphore_signal(barrier, inc=1, device_id=(pool, band), device_id_type=MESH)

    for pool in (near, far, beyond, before):
        hail(pool, n)
    for plane in range(ring):
        @pl.when(n == plane)
        def _():
            count = 4
            for other in (plane - 1, plane + 1):
                if 0 <= other < ring:
                    hail(near, other)
                    hail(me, other)
                    count += 2
            pl.semaphore_wait(barrier, count)

    def place(plane, band, kind):
        return visits(ring, plane).index((kind, band))

    def copy(half, source, step, pool, band, slot):
        return pltpu.make_async_remote_copy(
            src_ref=source.at[half],
            dst_ref=bufs.at[step, half],
            send_sem=send_sem.at[slot, half],
            recv_sem=recv_sem.at[step, half],
            device_id=(pool, band),
            device_id_type=MESH,
        )

    def own_sends(plane):
        found = [
            (sent_ref, place(plane, plane, 0), near, plane, 0),
            (sent_ref, place(plane, plane, 1), far, plane, 1),
        ]
        for other in (plane - 1, plane + 1):
            if 0 <= other < ring:
                found.append((sent_ref, place(other, plane, 0), near, other, len(found)))
        return found

    def later_sends(plane, parity):
        found, slot = {}, 4
        for step, (kind, band) in enumerate(visits(ring, plane)):
            found[step] = []
            for to_kind, pool, onward in forwards(ring, plane, parity, kind, band):
                target = me if pool == "me" else beyond
                found[step].append((bufs.at[step], place(onward, band, to_kind), target, onward, slot))
                slot += 1
        return found

    def classes(act):
        for plane in range(ring):
            for parity in range(2):
                pl.when(jnp.logical_and(n == plane, odd == parity))(functools.partial(act, plane, parity))

    def service(step, middle):
        def act(plane, parity):
            for when, events in moments(ring, plane, parity).items():
                if when % 2 == middle:

                    @pl.when(step == when // 2)
                    def _():
                        for kind, half, number, sends, band in events:
                            spot = bufs.at[number, half]
                            pltpu.make_async_copy(spot, spot, recv_sem.at[number, half]).wait()
                            for c in later_sends(plane, parity)[number]:
                                copy(half, *c).start()

        classes(act)

    def begin(plane, parity):
        for c in own_sends(plane):
            for half in range(2):
                copy(half, *c).start()

    classes(begin)

    lists = 0
    for plane in range(ring):
        bits = sum(kind << step for step, (kind, _) in enumerate(visits(ring, plane)))
        lists = lists + (n == plane).astype(jnp.int32) * bits

    lane = lax.broadcasted_iota(jnp.int32, (1, LANES), 1)
    sign = jnp.where(lane < HALF, 1.0, -1.0).astype(jnp.float32)
    scale = grid**1.5 / 16.0 / (grid * grid * grid)

    first = lane < HALF
    here = kpoint_coords(label_ref[me])
    column = lax.broadcasted_iota(jnp.int32, (grid, LANES), 0)
    for which, partner in enumerate((near, far)):
        there = kpoint_coords(label_ref[partner])
        off = [here[d] - there[d] for d in range(3)]
        plane_sum = squares(off[1], grid, column) + squares(off[2], grid, lane % HALF)

        def make_v(x, carry):
            shifted = (x - grid * (x // (grid // 2))).astype(jnp.float32) + off[0]
            edge = (x == grid // 2).astype(jnp.float32)
            total = plane_sum + (shifted * shifted + edge * FAR)
            v_ref[which, x] = jnp.where(total > 0.5 * FAR, 0.0, scale / total)
            return carry

        lax.fori_loop(0, grid, make_v, 0)

    def swap(x):
        return pltpu.roll(x, HALF, 1)

    def turned(x):
        return swap(x) * sign

    def tile(source, start):
        at, off = start // LANES, start % LANES
        halves = []
        for part in range(2):
            turn_by = (part * HALF - off) % LANES

            def lanes_of(column):
                x = source[part, :, column * LANES : (column + 1) * LANES].astype(jnp.float32)
                return pltpu.roll(x, turn_by, 1) if turn_by else x

            half = lanes_of(at)
            if off + grid > LANES:
                half = jnp.where(lane < part * HALF + LANES - off, half, lanes_of(at + 1))
            halves.append(half)
        return jnp.where(first, halves[0], halves[1])

    def along_lanes(x, which):
        high, low = split(x)
        out = jnp.dot(
            jnp.concatenate([high, low], axis=1), lanes_ref[which], preferred_element_type=jnp.float32
        )
        return out[:, :LANES] + out[:, LANES:]

    def along_rows(xs, sense):
        parts = []
        for x in xs:
            high, low = split(x)
            parts.append(jnp.concatenate([high, low, high], axis=0))
        outs = []
        for at in range(0, len(parts), 2):
            pair = jnp.concatenate(parts[at : at + 2], axis=1)
            out = jnp.dot(rows_ref[...], pair, preferred_element_type=jnp.float32)
            for j in range(len(parts[at : at + 2])):
                piece = out[:, j * LANES : (j + 1) * LANES]
                q = turned(piece[grid:])
                outs.append(piece[:grid] + q if sense > 0 else piece[:grid] - q)
        return outs

    def one_field(step, carry):
        service(step, 0)
        which = jnp.right_shift(lists, step) % 2
        source = bufs.at[step]

        for base in range(0, grid, batch):
            dens = []
            for y in range(base, base + batch):
                span = slice(y * grid, (y + 1) * grid)
                b = tile(source, y * grid)
                band[span, :] = b
                dens.append(b * a1_ref[span, :] + swap(b) * a2_ref[span, :])
            spec = along_lanes(jnp.concatenate(dens, axis=0), 0)
            outs = along_rows([spec[j * grid : (j + 1) * grid] for j in range(batch)], 1)
            for j in range(batch):
                field[(base + j) * pitch : (base + j) * pitch + grid, :] = outs[j]

        service(step, 1)

        for base in range(0, grid, batch):
            xs = [field[pl.ds(base + j, grid, stride=pitch), :] for j in range(batch)]
            spec = along_rows(xs, 1)
            spec = [spec[j] * v_ref[which, base + j] for j in range(batch)]
            outs = along_rows(spec, -1)
            for j in range(batch):
                field[pl.ds(base + j, grid, stride=pitch), :] = outs[j]

        for base in range(0, grid, batch):
            mids = [field[(base + j) * pitch : (base + j) * pitch + grid, :] for j in range(batch)]
            outs = along_rows(mids, -1)
            pot = along_lanes(jnp.concatenate(outs, axis=0), 1)
            for j in range(batch):
                y = base + j
                span = slice(y * grid, (y + 1) * grid)
                b = band[span, :]
                piece = pot[j * grid : (j + 1) * grid]
                acc1[span, :] = acc1[span, :] + b * piece
                acc2[span, :] = acc2[span, :] + b * swap(piece)
        return carry

    group = math.lcm(grid, LANES)
    lines = group // grid

    def prepare(g, carry):
        view = sent_ref.at[:, :, pl.ds(pl.multiple_of(g * group, LANES), group)]
        for j in range(lines):
            a = tile(view, j * grid)
            other = swap(a)
            rows = pl.ds(pl.multiple_of((g * lines + j) * grid, 8), grid)
            a1_ref[rows, :] = jnp.where(first, a, -other)
            a2_ref[rows, :] = jnp.where(first, other, a)
        return carry

    lax.fori_loop(0, grid // lines, prepare, 0)
    acc1[...] = jnp.zeros_like(acc1)
    acc2[...] = jnp.zeros_like(acc2)
    lax.fori_loop(0, 2 * ring, one_field, 0)

    def finish(g, carry):
        made = [[None] * (group // LANES) for _ in range(2)]
        for j in range(lines):
            rows = pl.ds(pl.multiple_of((g * lines + j) * grid, 8), grid)
            one = acc1[rows, :]
            two = acc2[rows, :]
            start = j * grid
            at, off = start // LANES, start % LANES
            for part, value in enumerate((one - swap(one), two + swap(two))):
                value = pltpu.roll(value, off, 1) if off else value
                row = made[part]
                row[at] = value if off == 0 else jnp.where(lane < off, row[at], value)
                if off + grid > LANES:
                    row[at + 1] = value
        for part in range(2):
            for at in range(group // LANES):
                lanes_at = pl.ds(pl.multiple_of(g * group + at * LANES, LANES), LANES)
                out_ref[part, :, lanes_at] = made[part][at]
        return carry

    lax.fori_loop(0, grid // lines, finish, 0)

    def settle(plane, parity):
        for copies in [own_sends(plane), *later_sends(plane, parity).values()]:
            for c in copies:
                for half in range(2):
                    copy(half, *c).wait_send()

    classes(settle)


def per_device(psi, kpoint_of_pool):
    own, own_bands = psi[0, :, 0], psi.shape[2]
    grid, points = own.shape[1], own.shape[2]
    ring = lax.axis_size("band")
    pools = lax.axis_size("kpool")
    lanes, rows = dft_tables(grid)
    whole = pl.BlockSpec(memory_space=pltpu.VMEM)
    pitch = grid + PITCH
    total = pl.pallas_call(
        functools.partial(kernel, grid, ring, pools, pitch, BATCH),
        in_specs=[pl.BlockSpec(memory_space=pltpu.SMEM)] + [whole] * 3,
        out_specs=whole,
        out_shape=pltpu.VMEM(own.shape, jnp.float32),
        scratch_shapes=[
            pltpu.VMEM((2 * ring,) + own.shape, jnp.bfloat16),
            pltpu.VMEM((grid * pitch, LANES), jnp.float32),
            pltpu.VMEM((points, LANES), jnp.float32),
            pltpu.VMEM((points, LANES), jnp.float32),
            pltpu.VMEM((points, LANES), jnp.float32),
            pltpu.VMEM((points, LANES), jnp.float32),
            pltpu.VMEM((points, LANES), jnp.float32),
            pltpu.VMEM((2, grid, grid, LANES), jnp.float32),
            pltpu.SemaphoreType.DMA((2 * ring, 2)),
            pltpu.SemaphoreType.DMA((4 + 3 * ring, 2)),
        ],
        compiler_params=pltpu.CompilerParams(collective_id=0, has_side_effects=True),
    )(kpoint_of_pool, own, jnp.asarray(lanes), jnp.asarray(rows))
    weight = -((2.0 * ROUNDS * ring * own_bands) ** (-0.5))
    return (total * weight)[None, :, None]


def solution(mesh):
    in_specs = (P("kpool", None, "band", None, None), P())
    out_specs = P("kpool", None, "band", None, None)
    return jax.shard_map(per_device, mesh=mesh, in_specs=in_specs, out_specs=out_specs, check_vma=False)
```
